32 devices in a mesh: section: 4 (over z), branch: 8 (over y, x, core).
Axes of the slice: x: 2, y: 2, z: 4, core: 2. Of those that a mesh axis runs over, the one named last changes fastest.
Arguments:
- layer_input: bfloat16 [4, 2, 1024, 4096], P('section', None, 'branch'), may hold values from -6 to 6
- cotangent: bfloat16 [2, 1024, 4096], P(None, 'branch'), may hold values from -6 to 6
- state_in: float32 [4, 2, 1024, 64], P('section', None, 'branch'), may hold values from -2 to 2
- state_out: float32 [4, 2, 1024, 64], P('section', None, 'branch'), may hold values from -2 to 2
- step_size: float32 [4, 2, 1024, 64], P('section', None, 'branch'), may hold values from 0.01 to 0.1
- saved_states: float32 [4, 2, 8, 64, 64, 64], P('section', None, 'branch'), may hold values from -6 to 6
- decay_rate: float32 [4, 64], P('section'), may hold values from 0.001 to 0.3
- skip_gain: float32 [4, 64], P('section'), may hold values from 0.5 to 1.5
- lengths: int32 [2, 4], replicated, may hold values from 32 to 128, as said below
Outputs:
- input_grad: bfloat16 [4, 2, 1024, 4096], P('section', None, 'branch')
- grad_state_in: float32 [4, 2, 1024, 64], P('section', None, 'branch')
- grad_state_out: float32 [4, 2, 1024, 64], P('section', None, 'branch')
- grad_step: float32 [4, 2, 1024, 64], P('section', None, 'branch')
- grad_decay: float32 [4, 64], P('section')
- grad_skip: float32 [4, 64], P('section')
The draws below stay inside these ranges and needn't reach their ends.
Inputs may be any that keep to these rules, and one draw needn't show every extreme that they name: lengths[m, j] counts the live tokens of completion j of family m; every family has a completion of exactly 128.
All inputs are finite; a program needn't handle non-finite values.
Results may differ from the reference program's by a relative error of at most 0.0058.
Values may be sent and summed in bfloat16 or wider, within the bound.
A program may use at most 384 MiB of HBM per device.

```python
import math
import jax
import jax.numpy as jnp
from jax import lax

HEADS = 64
HEADDIM = 64
STATE = 64
ROWS = 128
MICRO = 2
SECTIONS = 4
WIDTH = 4096
SEGMENTS = 8
COMPLETIONS = 4
TOKENS = 1024


def draw_lengths(key, part):
    first, second = jax.random.split(jax.random.fold_in(key, 17))
    values = jax.random.randint(first, (MICRO, COMPLETIONS), ROWS // 4, ROWS + 1)
    picked = jax.random.randint(second, (MICRO, 1), 0, COMPLETIONS)
    return jnp.where(jnp.arange(COMPLETIONS)[None, :] == picked, ROWS, values).astype(jnp.int32)


def block_scale(rng, dims, cuts, low, high):
    gain = 1.0
    for dim, parts in cuts:
        draws = jax.random.uniform(jax.random.fold_in(jax.random.fold_in(rng, 6), dim), (parts,), jnp.float32, low / len(cuts), high / len(cuts))
        gain = gain * jnp.repeat(jnp.exp(draws), dims[dim] // parts).reshape((-1,) + (1,) * (len(dims) - 1 - dim))
    return gain


def noise(stream_key, dims, width, limit, shards=(), dtype=jnp.bfloat16):
    entries = jax.random.normal(stream_key, dims, jnp.float32) * width
    if len(shards) > 0:
        entries = block_scale(stream_key, dims, shards, -0.22, 0.18) * entries
    return jnp.clip(entries, min=-limit, max=limit).astype(dtype)


def setup_inputs(seed: int = 0) -> dict:
    seeds = jax.random.split(jax.random.key(seed), 10)
    return {
        "layer_input": noise(seeds[0], (SECTIONS, MICRO, TOKENS, WIDTH), 1.0, 6.0, ((0, 4), (2, 8))),
        "cotangent": noise(seeds[1], (MICRO, TOKENS, WIDTH), 1.0, 6.0, ((1, 8),)),
        "state_in": noise(seeds[2], (SECTIONS, MICRO, TOKENS, STATE), 0.3, 2.0, ((0, 4), (2, 8)), jnp.float32),
        "state_out": noise(seeds[3], (SECTIONS, MICRO, TOKENS, STATE), 0.3, 2.0, ((0, 4), (2, 8)), jnp.float32),
        "step_size": jnp.clip(jnp.exp(math.log(0.1) - 2.3025851 * jax.random.uniform(seeds[4], (SECTIONS, MICRO, TOKENS, HEADS), jnp.float32) ** block_scale(seeds[4], (SECTIONS, MICRO, TOKENS, HEADS), ((0, 4), (2, 8)), -0.2, 0.2)), 0.01, 0.1),
        "saved_states": noise(seeds[5], (SECTIONS, MICRO, SEGMENTS, HEADS, HEADDIM, STATE), 1.0, 6.0, ((0, 4), (2, 8)), jnp.float32),
        "decay_rate": jnp.clip(jnp.exp(math.log(0.3) - 5.7037825 * jax.random.uniform(seeds[6], (SECTIONS, HEADS), jnp.float32) ** block_scale(seeds[6], (SECTIONS, HEADS), ((0, 4),), -0.2, 0.2)), 0.001, 0.3),
        "skip_gain": jnp.clip(1.0 + 0.1 * jax.random.normal(seeds[7], (SECTIONS, HEADS), jnp.float32), 0.5, 1.5),
        "lengths": draw_lengths(jax.random.fold_in(seeds[9], 71), 0),
    }


HIGH = lax.Precision.HIGHEST

def decay_logs(step_rows, decay_vec):
    return jnp.cumsum(-decay_vec[None, :] * step_rows, axis=0)

def start_grad(upstream, out_rows, logdec):
    carried = jnp.exp(logdec)
    begin_grad = jnp.einsum('thp,tn->hpn', upstream * carried[:, :, None], out_rows, precision=HIGH)
    return (jnp.exp(logdec[-1]), begin_grad)

def local_terms(layer_x, upstream, in_rows, out_rows, step_rows, logdec):
    row_count = layer_x.shape[0]
    causal = jnp.arange(row_count)[:, None] >= jnp.arange(row_count)[None, :]
    lograte = logdec.T
    spread = lograte[:, :, None] - lograte[:, None, :]
    kernel = jnp.where(causal[None], jnp.exp(jnp.where(causal[None], spread, 0.0)), 0.0)
    affinity = jnp.dot(out_rows, in_rows.T, precision=HIGH)
    weighted = kernel * affinity[None]
    pair_grad = jnp.einsum('thp,uhp->htu', upstream, layer_x, precision=HIGH)
    scaled = kernel * pair_grad * step_rows.T[:, None, :]
    back_x = jnp.einsum('htu,thp->uhp', weighted, upstream, precision=HIGH)
    back_in = jnp.einsum('htu,tn->un', scaled, out_rows, precision=HIGH)
    back_out = jnp.einsum('htu,un->tn', scaled, in_rows, precision=HIGH)
    mixed_terms = scaled * affinity[None]
    back_log = (lax.optimization_barrier(jnp.sum(mixed_terms, axis=2)) - lax.optimization_barrier(jnp.sum(mixed_terms, axis=1))).T
    return (back_x, back_in, back_out, back_log)

def finish(layer_x, upstream, in_rows, out_rows, step_rows, logdec, decay_vec, gain_vec, saved_state, end_grad, local_part):
    back_x, back_in, back_out, back_log = local_part
    row_count = layer_x.shape[0]
    carried = jnp.exp(logdec)
    remain = jnp.exp(logdec[-1][None, :] - logdec)
    end_in = jnp.einsum('un,hpn->uhp', in_rows, end_grad, precision=HIGH)
    state_pull = back_x + remain[:, :, None] * end_in
    input_grad = gain_vec[None, :, None] * upstream + step_rows[:, :, None] * state_pull
    end_x = jnp.einsum('uhp,hpn->uhn', layer_x, end_grad, precision=HIGH)
    grad_in = back_in + jnp.einsum('uh,uhn->un', step_rows * remain, end_x, precision=HIGH)
    up_saved = jnp.einsum('thp,hpn->thn', upstream, saved_state, precision=HIGH)
    grad_out = back_out + jnp.einsum('th,thn->tn', carried, up_saved, precision=HIGH)
    read_saved = jnp.einsum('tn,hpn->thp', out_rows, saved_state, precision=HIGH)
    end_flow = step_rows * remain * lax.optimization_barrier(jnp.sum(layer_x * end_in, axis=2))
    last_term = jnp.exp(logdec[-1]) * lax.optimization_barrier(jnp.sum(end_grad * saved_state, axis=(1, 2))) + lax.optimization_barrier(jnp.sum(end_flow, axis=0))
    is_last = jnp.arange(row_count) == row_count - 1
    grad_log = back_log + carried * lax.optimization_barrier(jnp.sum(upstream * read_saved, axis=2)) - end_flow
    grad_log = grad_log + jnp.where(is_last[:, None], last_term[None, :], 0.0)
    grad_rate = jnp.cumsum(grad_log[::-1], axis=0)[::-1]
    grad_step = lax.optimization_barrier(jnp.sum(layer_x * state_pull, axis=2)) - decay_vec[None, :] * grad_rate
    decay_part = lax.optimization_barrier(jnp.sum(-step_rows * grad_rate, axis=0))
    skip_part = lax.optimization_barrier(jnp.sum(layer_x * upstream, axis=(0, 2)))
    return (input_grad, grad_in, grad_out, grad_step, decay_part, skip_part)

def reference(layer_input, cotangent, state_in, state_out, step_size, saved_states, decay_rate, skip_gain, lengths):
    prompt = SEGMENTS - COMPLETIONS
    grad_scale = 1.0 / math.sqrt(MICRO * TOKENS * HEADDIM)
    live_rows = jnp.arange(ROWS)[None, None, :] < lengths[:, :, None]
    keep_rows = jnp.concatenate([jnp.ones((MICRO, prompt, ROWS), bool), live_rows], axis=1)
    upstream_all = cotangent.astype(jnp.float32).reshape(MICRO, SEGMENTS, ROWS, HEADS, HEADDIM)
    upstream_all = jnp.where(keep_rows[:, :, :, None, None], upstream_all, 0.0)
    outs_input = [None] * SECTIONS
    outs_in = [None] * SECTIONS
    outs_out = [None] * SECTIONS
    outs_step = [None] * SECTIONS
    outs_decay = [None] * SECTIONS
    outs_skip = [None] * SECTIONS
    for section_at in range(SECTIONS - 1, -1, -1):
        decay_vec = decay_rate[section_at]
        gain_vec = skip_gain[section_at]
        list_input, list_in, list_out, list_step = ([], [], [], [])
        decay_acc = jnp.zeros((HEADS,), jnp.float32)
        skip_acc = jnp.zeros((HEADS,), jnp.float32)
        next_upstream = []
        for micro_at in range(MICRO):
            layer_x = layer_input[section_at, micro_at].astype(jnp.float32).reshape(SEGMENTS, ROWS, HEADS, HEADDIM)
            in_rows = state_in[section_at, micro_at].reshape(SEGMENTS, ROWS, STATE)
            out_rows = state_out[section_at, micro_at].reshape(SEGMENTS, ROWS, STATE)
            step_rows = step_size[section_at, micro_at].reshape(SEGMENTS, ROWS, HEADS)
            upstream = upstream_all[micro_at]
            logs = jax.vmap(decay_logs, (0, None))(step_rows, decay_vec)
            totals, begins = jax.vmap(start_grad)(upstream, out_rows, logs)
            fork_grad = lax.optimization_barrier(jnp.sum(begins[prompt:], axis=0))

            def chain_step(carry_grad, pieces):
                decay_total, begin_grad = pieces
                return (decay_total[:, None, None] * carry_grad + begin_grad, carry_grad)
            _, prompt_ends = lax.scan(chain_step, fork_grad, (totals[:prompt], begins[:prompt]), reverse=True)
            ends = jnp.concatenate([prompt_ends, jnp.zeros((COMPLETIONS, HEADS, HEADDIM, STATE), jnp.float32)], axis=0)

            def segment(pieces):
                seg_x, seg_up, seg_in, seg_out, seg_step, seg_log, seg_saved, seg_end = pieces
                local_part = local_terms(seg_x, seg_up, seg_in, seg_out, seg_step, seg_log)
                return finish(seg_x, seg_up, seg_in, seg_out, seg_step, seg_log, decay_vec, gain_vec, seg_saved, seg_end, local_part)
            results = lax.map(segment, (layer_x, upstream, in_rows, out_rows, step_rows, logs, saved_states[section_at, micro_at], ends))
            rounded = results[0].astype(jnp.bfloat16)
            list_input.append(rounded.reshape(TOKENS, WIDTH))
            list_in.append(results[1].reshape(TOKENS, STATE))
            list_out.append(results[2].reshape(TOKENS, STATE))
            list_step.append(results[3].reshape(TOKENS, HEADS))
            decay_acc = decay_acc + lax.optimization_barrier(jnp.sum(results[4], axis=0))
            skip_acc = skip_acc + lax.optimization_barrier(jnp.sum(results[5], axis=0))
            next_upstream.append(rounded.astype(jnp.float32))
        upstream_all = jnp.stack(next_upstream).reshape(MICRO, SEGMENTS, ROWS, HEADS, HEADDIM)
        outs_input[section_at] = jnp.stack(list_input)
        outs_in[section_at] = jnp.stack(list_in)
        outs_out[section_at] = jnp.stack(list_out)
        outs_step[section_at] = jnp.stack(list_step)
        outs_decay[section_at] = decay_acc * grad_scale
        outs_skip[section_at] = skip_acc * grad_scale
    return (jnp.stack(outs_input), jnp.stack(outs_in), jnp.stack(outs_out), jnp.stack(outs_step), jnp.stack(outs_decay), jnp.stack(outs_skip))
```

```python
import functools
import math

import jax
import jax.numpy as jnp
from jax import lax
from jax.experimental import pallas as pl
from jax.experimental.pallas import tpu as pltpu
from jax.sharding import PartitionSpec as P

HIGH = lax.Precision.HIGHEST
F32 = jnp.float32
BF16 = jnp.bfloat16
MESH = pl.DeviceIdType.MESH


def nn(a, b, precision=None):
    return lax.dot_general(
        a, b, (((1,), (0,)), ((), ())), precision=precision, preferred_element_type=F32
    )


def nt(a, b, precision=None):
    return lax.dot_general(
        a, b, (((1,), (1,)), ((), ())), precision=precision, preferred_element_type=F32
    )


def split(value):
    high = value.astype(BF16)
    return high, (value - high.astype(F32)).astype(BF16)


def window(
    sections,
    branches,
    lanes,
    grad_scale,
    lengths,
    layer_x,
    cotangent,
    state_in,
    state_out,
    step_size,
    saved,
    decay,
    gain,
    out_x,
    out_in,
    out_out,
    out_step,
    out_decay,
    out_skip,
    up_buf,
    end_buf,
    end_send,
    rates,
    gains,
    pull_mix,
    in_mix,
    read_mix,
    saved_mix,
    out_turn,
    pairs,
    acc_read,
    acc_pull,
    acc_last,
    end_acc,
    shares,
    up_sem,
    up_send_sem,
    end_sem,
    end_send_sem,
    share_sem,
    share_send_sem,
):
    section_at = lax.axis_index("section")
    branch_at = lax.axis_index("branch")
    half = branches // 2
    micros, rows, width = layer_x.shape
    states = state_in.shape[2]
    heads = decay.shape[1]
    size = width // heads
    pieces = width // lanes
    group = lanes // size
    chunks = micros * pieces
    is_completion = branch_at >= half
    is_top = section_at == sections - 1

    def place(k):
        m = k // pieces
        c = k % pieces
        return m, c, pl.multiple_of(c * lanes, lanes)

    def top_copy(k):
        m, c, at = place(k)
        return pltpu.make_async_copy(
            cotangent.at[m, :, pl.ds(at, lanes)], up_buf.at[k], up_sem.at[k]
        )

    def down_copy(k):
        m, c, at = place(k)
        return pltpu.make_async_remote_copy(
            src_ref=out_x.at[m, :, pl.ds(at, lanes)],
            dst_ref=up_buf.at[k],
            send_sem=up_send_sem.at[k],
            recv_sem=up_sem.at[k],
            device_id=(lax.rem(section_at + sections - 1, sections), branch_at),
            device_id_type=MESH,
        )

    def end_copy(k, slot, target):
        return pltpu.make_async_remote_copy(
            src_ref=end_send.at[k],
            dst_ref=end_buf.at[slot, k],
            send_sem=end_send_sem.at[k],
            recv_sem=end_sem.at[slot, k],
            device_id=(section_at, target),
            device_id_type=MESH,
        )

    @pl.when(is_top)
    def _():
        def begin(k, carry):
            top_copy(k).start()
            return carry

        lax.fori_loop(0, chunks, begin, 0)

    barrier = pltpu.get_barrier_semaphore()
    for by in (1, sections - 1):
        pl.semaphore_signal(
            barrier,
            inc=1,
            device_id=(lax.rem(section_at + by, sections), branch_at),
            device_id_type=MESH,
        )
    for by in range(1, branches):
        pl.semaphore_signal(
            barrier,
            inc=1,
            device_id=(section_at, lax.rem(branch_at + by, branches)),
            device_id_type=MESH,
        )

    row_at = lax.broadcasted_iota(jnp.int32, (rows, rows), 0)
    col_at = lax.broadcasted_iota(jnp.int32, (rows, rows), 1)
    lower = row_at >= col_at
    upper = row_at <= col_at
    unit = (
        lax.broadcasted_iota(jnp.int32, (states, states), 0)
        == lax.broadcasted_iota(jnp.int32, (states, states), 1)
    ).astype(BF16)
    for m in range(micros):
        step = step_size[m]
        logs = nn(lower.astype(F32), -decay[...] * step, HIGH)
        high, low = split(jnp.exp(logs))
        rates[m, 0, :rows] = high
        rates[m, 1, :rows] = low
        high, low = split(step * jnp.exp(-logs))
        rates[m, 0, rows:] = high
        rates[m, 1, rows:] = low
        b, c = state_in[m], state_out[m]
        pull_mix[m] = jnp.where(upper, nt(b, c, HIGH), 0.0).astype(BF16)
        in_mix[m] = b.astype(BF16)
        read_mix[m, :rows] = jnp.where(lower, nt(c, b, HIGH), 0.0).astype(BF16)
        read_mix[m, rows:] = nt(unit, b.astype(BF16)).astype(BF16)
        saved_mix[m, :rows] = c.astype(BF16)
        saved_mix[m, rows:] = unit
        out_turn[m] = nt(unit, c.astype(BF16)).astype(BF16)
    high, low = split(jnp.broadcast_to(gain[...], (16, heads)))
    gains[0] = high
    gains[1] = low
    out_in[...] = jnp.zeros_like(out_in)
    out_out[...] = jnp.zeros_like(out_out)
    pairs[...] = jnp.zeros_like(pairs)
    acc_read[...] = jnp.zeros_like(acc_read)
    acc_pull[...] = jnp.zeros_like(acc_pull)
    acc_last[...] = jnp.zeros_like(acc_last)
    end_acc[...] = jnp.zeros_like(end_acc)

    pl.semaphore_wait(barrier, branches + 1)

    def chunk(k, carry):
        m, c, at = place(k)
        spread = (
            lax.broadcasted_iota(jnp.int32, (heads, lanes), 0)
            == c * group + lax.broadcasted_iota(jnp.int32, (heads, lanes), 1) // size
        ).astype(BF16)
        wide = nn(rates[m, 0], spread) + nn(rates[m, 1], spread)
        gain_wide = (nn(gains[0], spread) + nn(gains[1], spread))[0:1]
        carried = wide[:rows]
        drive = wide[rows:]
        total = carried[rows - 1 :]
        x = layer_x[m, :, pl.ds(at, lanes)].astype(F32)
        fed = (x * drive).astype(BF16)

        @pl.when(is_top)
        def _():
            top_copy(k).wait()

        @pl.when(jnp.logical_not(is_top))
        def _():
            down_copy(k).wait_recv()

        limit = jnp.where(
            is_top & is_completion, lengths[m, jnp.maximum(branch_at - half, 0)], rows
        )
        live = lax.broadcasted_iota(jnp.int32, (rows, lanes), 0) < limit
        up = jnp.where(live, up_buf[k].astype(F32), 0.0)
        up_carried = (up * carried).astype(BF16)
        begin = nn(out_turn[m], up_carried)

        @pl.when(branch_at == half - 1)
        def _():
            for slot in range(half):
                end_copy(k, slot, half - 1).wait_recv()
            end = end_buf[0, k].astype(F32)
            for slot in range(1, half):
                end = end + end_buf[slot, k].astype(F32)
            end_acc[...] = end

        @pl.when(branch_at < half - 1)
        def _():
            end_copy(k, 0, half - 1).wait_recv()
            end_acc[...] = end_buf[0, k].astype(F32)

        end = total * end_acc[...]
        end_send[k] = (begin + end).astype(BF16)

        @pl.when(branch_at > 0)
        def _():
            slot = jnp.maximum(branch_at - half, 0)
            end_copy(k, slot, jnp.minimum(branch_at - 1, half - 1)).start()

        end = end.astype(BF16)
        pull = nn(pull_mix[m], up_carried) + nn(in_mix[m], end)
        out_x[m, :, pl.ds(at, lanes)] = (gain_wide * up + drive * pull).astype(BF16)

        @pl.when(section_at > 0)
        def _():
            down_copy(k).start()

        kept = saved[m, pl.ds(at, lanes), :].astype(BF16)
        read = nn(read_mix[m], fed) + nt(saved_mix[m], kept)
        pairs[m] += nt(fed, up_carried)
        out_in[m] += nt(fed, end)
        out_out[m] += nn(up_carried, kept)
        high, low = split(up_carried.astype(F32) * read[:rows])
        acc_read[m] += nt(high, spread) + nt(low, spread)
        high, low = split(fed.astype(F32) * pull)
        acc_pull[m] += nt(high, spread) + nt(low, spread)
        last = jnp.sum(end.astype(F32) * read[rows:], axis=0, keepdims=True)
        skip = jnp.sum(x * up, axis=0, keepdims=True)
        high, low = split(
            jnp.concatenate(
                [jnp.broadcast_to(last, (8, lanes)), jnp.broadcast_to(skip, (8, lanes))], axis=0
            )
        )
        acc_last[m] += nt(high, spread) + nt(low, spread)
        return carry

    lax.fori_loop(0, chunks, chunk, 0)

    decay_sum = jnp.zeros((1, heads), F32)
    skip_sum = jnp.zeros((1, heads), F32)
    for m in range(micros):
        step = step_size[m]
        flow = acc_read[m] - acc_pull[m]
        grad_rate = nn(upper.astype(F32), flow, HIGH) + acc_last[m, 0:1]
        out_step[m] = acc_pull[m] / step - decay[...] * grad_rate
        decay_sum = decay_sum - jnp.sum(step * grad_rate, axis=0, keepdims=True)
        skip_sum = skip_sum + acc_last[m, 8:9]
    shares[branch_at] = jnp.concatenate(
        [jnp.broadcast_to(decay_sum, (8, heads)), jnp.broadcast_to(skip_sum, (8, heads))], axis=0
    )

    def share_copy(by):
        return pltpu.make_async_remote_copy(
            src_ref=shares.at[branch_at],
            dst_ref=shares.at[branch_at],
            send_sem=share_send_sem.at[by],
            recv_sem=share_sem.at[by],
            device_id=(section_at, lax.rem(branch_at + by, branches)),
            device_id_type=MESH,
        )

    def share_arrival(by):
        slot = lax.rem(branch_at + branches - by, branches)
        return pltpu.make_async_remote_copy(
            src_ref=shares.at[slot],
            dst_ref=shares.at[slot],
            send_sem=share_send_sem.at[by],
            recv_sem=share_sem.at[by],
            device_id=(section_at, lax.rem(branch_at + by, branches)),
            device_id_type=MESH,
        )

    for by in range(1, branches):
        share_copy(by).start()

    for m in range(micros):
        kept = jnp.where(upper, pairs[m], 0.0)
        turned = nt((row_at == col_at).astype(F32), kept, HIGH)
        out_in[m] += nn(kept, state_out[m], HIGH)
        out_out[m] += nn(turned, state_in[m], HIGH)

    def drain(k, carry):
        @pl.when(branch_at > 0)
        def _():
            end_copy(k, 0, half - 1).wait_send()

        @pl.when(section_at > 0)
        def _():
            down_copy(k).wait_send()

        return carry

    lax.fori_loop(0, chunks, drain, 0)
    for by in range(1, branches):
        share_copy(by).wait_send()
        share_arrival(by).wait_recv()
    share = shares[0]
    for at in range(1, branches):
        share = share + shares[at]
    share = share * grad_scale
    out_decay[...] = share[0:1]
    out_skip[...] = share[8:9]


def shards(
    layer_input,
    cotangent,
    state_in,
    state_out,
    step_size,
    saved_states,
    decay_rate,
    skip_gain,
    lengths,
):
    sections = lax.axis_size("section")
    branches = lax.axis_size("branch")
    _, micros, rows, width = layer_input.shape
    heads = decay_rate.shape[1]
    states = state_in.shape[3]
    size = width // heads
    group = math.gcd(heads, 8)
    lanes = group * size
    chunks = micros * (width // lanes)
    half = branches // 2
    grad_scale = 1.0 / math.sqrt(micros * rows * branches * size)
    vmem = pl.BlockSpec(memory_space=pltpu.VMEM)
    outs = pl.pallas_call(
        functools.partial(window, sections, branches, lanes, grad_scale),
        out_shape=(
            jax.ShapeDtypeStruct((micros, rows, width), BF16),
            jax.ShapeDtypeStruct((micros, rows, states), F32),
            jax.ShapeDtypeStruct((micros, rows, states), F32),
            jax.ShapeDtypeStruct((micros, rows, heads), F32),
            jax.ShapeDtypeStruct((1, heads), F32),
            jax.ShapeDtypeStruct((1, heads), F32),
        ),
        in_specs=[
            pl.BlockSpec(memory_space=pltpu.SMEM),
            vmem,
            pl.BlockSpec(memory_space=pl.ANY),
            vmem,
            vmem,
            vmem,
            vmem,
            vmem,
            vmem,
        ],
        out_specs=[vmem] * 6,
        scratch_shapes=[
            pltpu.VMEM((chunks, rows, lanes), BF16),
            pltpu.VMEM((half, chunks, states, lanes), BF16),
            pltpu.VMEM((chunks, states, lanes), BF16),
            pltpu.VMEM((micros, 2, 2 * rows, heads), BF16),
            pltpu.VMEM((2, 16, heads), BF16),
            pltpu.VMEM((micros, rows, rows), BF16),
            pltpu.VMEM((micros, rows, states), BF16),
            pltpu.VMEM((micros, rows + states, rows), BF16),
            pltpu.VMEM((micros, rows + states, states), BF16),
            pltpu.VMEM((micros, states, rows), BF16),
            pltpu.VMEM((micros, rows, rows), F32),
            pltpu.VMEM((micros, rows, heads), F32),
            pltpu.VMEM((micros, rows, heads), F32),
            pltpu.VMEM((micros, 16, heads), F32),
            pltpu.VMEM((states, lanes), F32),
            pltpu.VMEM((branches, 16, heads), F32),
            pltpu.SemaphoreType.DMA((chunks,)),
            pltpu.SemaphoreType.DMA((chunks,)),
            pltpu.SemaphoreType.DMA((half, chunks)),
            pltpu.SemaphoreType.DMA((chunks,)),
            pltpu.SemaphoreType.DMA((branches,)),
            pltpu.SemaphoreType.DMA((branches,)),
        ],
        compiler_params=pltpu.CompilerParams(
            collective_id=0, has_side_effects=True, vmem_limit_bytes=50 * 1024 * 1024
        ),
        name="window",
    )(
        lengths,
        layer_input[0],
        cotangent,
        state_in[0],
        state_out[0],
        step_size[0],
        saved_states.reshape(micros, width, states),
        decay_rate,
        skip_gain,
    )
    return (outs[0][None], outs[1][None], outs[2][None], outs[3][None], outs[4], outs[5])


def solution(mesh):
    layered = P("section", None, "branch", None)
    return jax.shard_map(
        shards,
        mesh=mesh,
        in_specs=(
            layered,
            P(None, "branch", None),
            layered,
            layered,
            layered,
            P("section", None, "branch", None, None, None),
            P("section", None),
            P("section", None),
            P(),
        ),
        out_specs=(
            layered,
            layered,
            layered,
            layered,
            P("section", None),
            P("section", None),
        ),
        check_vma=False,
    )
```

```python
import functools
import math

import jax
import jax.numpy as jnp
from jax import lax
from jax.experimental import pallas as pl
from jax.experimental.pallas import tpu as pltpu
from jax.sharding import PartitionSpec as P

HIGH = lax.Precision.HIGHEST
F32 = jnp.float32
BF16 = jnp.bfloat16
MESH = pl.DeviceIdType.MESH


def nn(a, b, precision=None):
    return lax.dot_general(
        a, b, (((1,), (0,)), ((), ())), precision=precision, preferred_element_type=F32
    )


def nt(a, b, precision=None):
    return lax.dot_general(
        a, b, (((1,), (1,)), ((), ())), precision=precision, preferred_element_type=F32
    )


def split(value):
    high = value.astype(BF16)
    return high, (value - high.astype(F32)).astype(BF16)


def window(
    sections,
    branches,
    lanes,
    grad_scale,
    lengths_hbm,
    x_hbm,
    cotangent,
    state_in,
    state_out,
    step_size,
    saved_hbm,
    decay_hbm,
    gain_hbm,
    out_x,
    out_in,
    out_out,
    out_step,
    out_decay,
    out_skip,
    lengths,
    layer_x,
    saved,
    decay,
    gain,
    up_buf,
    end_buf,
    end_send,
    chain_buf,
    chain_send,
    mixed,
    rates,
    gains,
    pull_mix,
    read_mix,
    saved_mix,
    out_turn,
    pairs,
    acc_read,
    acc_pull,
    acc_last,
    in_acc,
    out_acc,
    end_acc,
    shares,
    load_sem,
    big_sem,
    up_sem,
    up_send_sem,
    end_sem,
    end_send_sem,
    chain_sem,
    chain_send_sem,
    share_sem,
    share_send_sem,
):
    section_at = lax.axis_index("section")
    branch_at = lax.axis_index("branch")
    half = branches // 2
    micros, rows, width = layer_x.shape
    states = state_in.shape[1]
    heads = decay.shape[1]
    size = width // heads
    pieces = width // lanes
    group = lanes // size
    chunks = micros * pieces
    is_completion = branch_at >= half
    is_top = section_at == sections - 1

    def place(k):
        m = k // pieces
        c = k % pieces
        return m, c, pl.multiple_of(c * lanes, lanes)

    def top_copy(k):
        m, c, at = place(k)
        return pltpu.make_async_copy(
            cotangent.at[m, :, pl.ds(at, lanes)], up_buf.at[k], up_sem.at[k]
        )

    def down_copy(k):
        m, c, at = place(k)
        return pltpu.make_async_remote_copy(
            src_ref=out_x.at[m, :, pl.ds(at, lanes)],
            dst_ref=up_buf.at[k],
            send_sem=up_send_sem.at[k],
            recv_sem=up_sem.at[k],
            device_id=(lax.rem(section_at + sections - 1, sections), branch_at),
            device_id_type=MESH,
        )

    def end_copy(k, slot):
        return pltpu.make_async_remote_copy(
            src_ref=end_send.at[k],
            dst_ref=end_buf.at[slot, k],
            send_sem=end_send_sem.at[k],
            recv_sem=end_sem.at[slot, k],
            device_id=(section_at, half - 1),
            device_id_type=MESH,
        )

    def chain_copy(k):
        return pltpu.make_async_remote_copy(
            src_ref=chain_send.at[k],
            dst_ref=chain_buf.at[k],
            send_sem=chain_send_sem.at[k],
            recv_sem=chain_sem.at[k],
            device_id=(section_at, jnp.maximum(branch_at - 1, 0)),
            device_id_type=MESH,
        )

    def x_copy(m):
        return pltpu.make_async_copy(x_hbm.at[m], layer_x.at[m], big_sem.at[m, 0])

    def saved_copy(m):
        return pltpu.make_async_copy(saved_hbm.at[m], saved.at[m], big_sem.at[m, 1])

    small = (
        pltpu.make_async_copy(decay_hbm, decay, load_sem.at[0]),
        pltpu.make_async_copy(gain_hbm, gain, load_sem.at[1]),
        pltpu.make_async_copy(lengths_hbm, lengths, load_sem.at[2]),
    )
    for copy in small:
        copy.start()

    @pl.when(is_top)
    def _():
        def begin(k, carry):
            top_copy(k).start()
            return carry

        lax.fori_loop(0, chunks, begin, 0)

    for m in range(micros):
        x_copy(m).start()
        saved_copy(m).start()

    barrier = pltpu.get_barrier_semaphore()
    for by in (1, sections - 1):
        pl.semaphore_signal(
            barrier,
            inc=1,
            device_id=(lax.rem(section_at + by, sections), branch_at),
            device_id_type=MESH,
        )
    for by in range(1, branches):
        pl.semaphore_signal(
            barrier,
            inc=1,
            device_id=(section_at, lax.rem(branch_at + by, branches)),
            device_id_type=MESH,
        )

    row_at = lax.broadcasted_iota(jnp.int32, (rows, rows), 0)
    col_at = lax.broadcasted_iota(jnp.int32, (rows, rows), 1)
    lower = row_at >= col_at
    upper = row_at <= col_at
    unit = (
        lax.broadcasted_iota(jnp.int32, (states, states), 0)
        == lax.broadcasted_iota(jnp.int32, (states, states), 1)
    ).astype(BF16)
    for copy in small:
        copy.wait()
    for m in range(micros):
        step = step_size[m].T
        logs = nn(lower.astype(F32), -decay[...] * step, HIGH)
        high, low = split(jnp.exp(logs))
        rates[m, :rows, :heads] = high
        rates[m, :rows, heads:] = low
        high, low = split(step * jnp.exp(-logs))
        rates[m, rows:, :heads] = high
        rates[m, rows:, heads:] = low
        b, c = state_in[m].T, state_out[m].T
        pull_mix[m, :, :rows] = jnp.where(upper, nt(b, c, HIGH), 0.0).astype(BF16)
        pull_mix[m, :, rows : rows + states] = b.astype(BF16)
        pull_mix[m, :, rows + states :] = b.astype(BF16)
        read_mix[m, :rows] = jnp.where(lower, nt(c, b, HIGH), 0.0).astype(BF16)
        read_mix[m, rows:] = state_in[m].astype(BF16)
        saved_mix[m, :rows] = c.astype(BF16)
        saved_mix[m, rows:] = unit
        high, low = split(state_out[m])
        out_turn[m, 0] = high
        out_turn[m, 1] = low
    high, low = split(jnp.broadcast_to(gain[...], (16, heads)))
    gains[:, :heads] = high
    gains[:, heads:] = low
    in_acc[...] = jnp.zeros_like(in_acc)
    out_acc[...] = jnp.zeros_like(out_acc)
    pairs[...] = jnp.zeros_like(pairs)
    acc_read[...] = jnp.zeros_like(acc_read)
    acc_pull[...] = jnp.zeros_like(acc_pull)
    acc_last[...] = jnp.zeros_like(acc_last)
    end_acc[...] = jnp.zeros_like(end_acc)

    pl.semaphore_wait(barrier, branches + 1)

    def chunk(k, carry):
        m, c, at = place(k)
        head = c * group
        spread = (
            lax.rem(lax.broadcasted_iota(jnp.int32, (2 * heads, lanes), 0), heads)
            == head + lax.broadcasted_iota(jnp.int32, (2 * heads, lanes), 1) // size
        ).astype(BF16)
        gather = (
            head + lax.broadcasted_iota(jnp.int32, (lanes, heads), 0) // size
            == lax.broadcasted_iota(jnp.int32, (lanes, heads), 1)
        ).astype(BF16)
        wide = nn(rates[m], spread)
        gain_wide = nn(gains[...], spread)[0:1]
        carried = wide[:rows]
        drive = wide[rows:]
        total = carried[rows - 1 :]

        @pl.when(is_top)
        def _():
            top_copy(k).wait()

        @pl.when(jnp.logical_not(is_top))
        def _():
            down_copy(k).wait_recv()

        limit = jnp.where(
            is_top & is_completion, lengths[m, jnp.maximum(branch_at - half, 0)], rows
        )
        live = lax.broadcasted_iota(jnp.int32, (rows, lanes), 0) < limit
        up = jnp.where(live, up_buf[k].astype(F32), 0.0)
        up_carried, up_low = split(up * carried)
        begin = (
            nn(out_turn[m, 0], up_carried)
            + nn(out_turn[m, 1], up_carried)
            + nn(out_turn[m, 0], up_low)
        )

        @pl.when(is_completion)
        def _():
            end_send[k] = begin.astype(BF16)
            end_copy(k, branch_at - half).start()

        @pl.when(branch_at == half - 1)
        def _():
            for slot in range(half):
                end_copy(k, slot).wait_recv()
            end = end_buf[0, k].astype(F32)
            for slot in range(1, half):
                end = end + end_buf[slot, k].astype(F32)
            end_acc[...] = end

        @pl.when(branch_at < half - 1)
        def _():
            chain_copy(k).wait_recv()
            end_acc[...] = chain_buf[k]

        end_full = total * end_acc[...]

        @pl.when((branch_at > 0) & (branch_at < half))
        def _():
            chain_send[k] = begin + end_full
            chain_copy(k).start()

        end, end_low = split(end_full)
        mixed[:rows] = up_carried
        mixed[rows : rows + states] = end
        mixed[rows + states :] = end_low
        pull = nn(pull_mix[m], mixed[...])
        out_x[m, :, pl.ds(at, lanes)] = (gain_wide * up + drive * pull).astype(BF16)

        @pl.when(section_at > 0)
        def _():
            down_copy(k).start()

        @pl.when(c == 0)
        def _():
            x_copy(m).wait()
            saved_copy(m).wait()

        x = layer_x[m, :, pl.ds(at, lanes)].astype(F32)
        fed = (x * drive).astype(BF16)
        kept = saved[m, pl.ds(at, lanes), :].astype(BF16)
        read = nn(read_mix[m], fed) + nt(saved_mix[m], kept)
        pairs[m] += nt(fed, up_carried)
        in_acc[m] += nt(fed, end)
        out_acc[m] += nn(up_carried, kept)
        high, low = split(up_carried.astype(F32) * read[:rows])
        acc_read[m] += nn(high, gather) + nn(low, gather)
        high, low = split(fed.astype(F32) * pull)
        acc_pull[m] += nn(high, gather) + nn(low, gather)
        last = jnp.sum(end.astype(F32) * read[rows:], axis=0, keepdims=True)
        skip = jnp.sum(x * up, axis=0, keepdims=True)
        high, low = split(
            jnp.concatenate(
                [jnp.broadcast_to(last, (8, lanes)), jnp.broadcast_to(skip, (8, lanes))], axis=0
            )
        )
        acc_last[m] += nn(high, gather) + nn(low, gather)
        return carry

    lax.fori_loop(0, chunks, chunk, 0)

    decay_sum = jnp.zeros((1, heads), F32)
    skip_sum = jnp.zeros((1, heads), F32)
    for m in range(micros):
        step = step_size[m].T
        flow = acc_read[m] - acc_pull[m]
        grad_rate = nn(upper.astype(F32), flow, HIGH) + acc_last[m, 0:1]
        out_step[m] = (acc_pull[m] / step - decay[...] * grad_rate).T
        decay_sum = decay_sum - jnp.sum(step * grad_rate, axis=0, keepdims=True)
        skip_sum = skip_sum + acc_last[m, 8:9]
    shares[branch_at] = jnp.concatenate(
        [jnp.broadcast_to(decay_sum, (8, heads)), jnp.broadcast_to(skip_sum, (8, heads))], axis=0
    )

    def share_copy(by):
        return pltpu.make_async_remote_copy(
            src_ref=shares.at[branch_at],
            dst_ref=shares.at[branch_at],
            send_sem=share_send_sem.at[by],
            recv_sem=share_sem.at[by],
            device_id=(section_at, lax.rem(branch_at + by, branches)),
            device_id_type=MESH,
        )

    def share_arrival(by):
        slot = lax.rem(branch_at + branches - by, branches)
        return pltpu.make_async_remote_copy(
            src_ref=shares.at[slot],
            dst_ref=shares.at[slot],
            send_sem=share_send_sem.at[by],
            recv_sem=share_sem.at[by],
            device_id=(section_at, lax.rem(branch_at + by, branches)),
            device_id_type=MESH,
        )

    for by in range(1, branches):
        share_copy(by).start()

    for m in range(micros):
        kept = jnp.where(upper, pairs[m], 0.0)
        out_in[m] = (in_acc[m] + nn(kept, state_out[m].T, HIGH)).T
        out_out[m] = out_acc[m].T + nn(state_in[m], kept, HIGH)

    def drain(k, carry):
        @pl.when(is_completion)
        def _():
            end_copy(k, 0).wait_send()

        @pl.when((branch_at > 0) & (branch_at < half))
        def _():
            chain_copy(k).wait_send()

        @pl.when(section_at > 0)
        def _():
            down_copy(k).wait_send()

        return carry

    lax.fori_loop(0, chunks, drain, 0)
    for by in range(1, branches):
        share_copy(by).wait_send()
        share_arrival(by).wait_recv()
    share = shares[0]
    for at in range(1, branches):
        share = share + shares[at]
    share = share * grad_scale
    out_decay[...] = share[0:1]
    out_skip[...] = share[8:9]


def shards(
    layer_input,
    cotangent,
    state_in,
    state_out,
    step_size,
    saved_states,
    decay_rate,
    skip_gain,
    lengths,
):
    sections = lax.axis_size("section")
    branches = lax.axis_size("branch")
    _, micros, rows, width = layer_input.shape
    heads = decay_rate.shape[1]
    states = state_in.shape[3]
    size = width // heads
    group = math.gcd(heads, 4)
    lanes = group * size
    chunks = micros * (width // lanes)
    half = branches // 2
    grad_scale = 1.0 / math.sqrt(micros * rows * branches * size)
    vmem = pl.BlockSpec(memory_space=pltpu.VMEM)
    hbm = pl.BlockSpec(memory_space=pltpu.HBM)
    outs = pl.pallas_call(
        functools.partial(window, sections, branches, lanes, grad_scale),
        out_shape=(
            jax.ShapeDtypeStruct((micros, rows, width), BF16),
            jax.ShapeDtypeStruct((micros, states, rows), F32),
            jax.ShapeDtypeStruct((micros, states, rows), F32),
            jax.ShapeDtypeStruct((micros, heads, rows), F32),
            jax.ShapeDtypeStruct((1, heads), F32),
            jax.ShapeDtypeStruct((1, heads), F32),
        ),
        in_specs=[hbm, hbm, hbm, vmem, vmem, vmem, hbm, hbm, hbm],
        out_specs=[vmem] * 6,
        scratch_shapes=[
            pltpu.SMEM(lengths.shape, jnp.int32),
            pltpu.VMEM((micros, rows, width), BF16),
            pltpu.VMEM((micros, width, states), F32),
            pltpu.VMEM((1, heads), F32),
            pltpu.VMEM((1, heads), F32),
            pltpu.VMEM((chunks, rows, lanes), BF16),
            pltpu.VMEM((half, chunks, states, lanes), BF16),
            pltpu.VMEM((chunks, states, lanes), BF16),
            pltpu.VMEM((chunks, states, lanes), F32),
            pltpu.VMEM((chunks, states, lanes), F32),
            pltpu.VMEM((rows + 2 * states, lanes), BF16),
            pltpu.VMEM((micros, 2 * rows, 2 * heads), BF16),
            pltpu.VMEM((16, 2 * heads), BF16),
            pltpu.VMEM((micros, rows, rows + 2 * states), BF16),
            pltpu.VMEM((micros, rows + states, rows), BF16),
            pltpu.VMEM((micros, rows + states, states), BF16),
            pltpu.VMEM((micros, 2, states, rows), BF16),
            pltpu.VMEM((micros, rows, rows), F32),
            pltpu.VMEM((micros, rows, heads), F32),
            pltpu.VMEM((micros, rows, heads), F32),
            pltpu.VMEM((micros, 16, heads), F32),
            pltpu.VMEM((micros, rows, states), F32),
            pltpu.VMEM((micros, rows, states), F32),
            pltpu.VMEM((states, lanes), F32),
            pltpu.VMEM((branches, 16, heads), F32),
            pltpu.SemaphoreType.DMA((3,)),
            pltpu.SemaphoreType.DMA((micros, 2)),
            pltpu.SemaphoreType.DMA((chunks,)),
            pltpu.SemaphoreType.DMA((chunks,)),
            pltpu.SemaphoreType.DMA((half, chunks)),
            pltpu.SemaphoreType.DMA((chunks,)),
            pltpu.SemaphoreType.DMA((chunks,)),
            pltpu.SemaphoreType.DMA((chunks,)),
            pltpu.SemaphoreType.DMA((branches,)),
            pltpu.SemaphoreType.DMA((branches,)),
        ],
        compiler_params=pltpu.CompilerParams(
            collective_id=0, has_side_effects=True, vmem_limit_bytes=67_043_328
        ),
        name="window",
    )(
        lengths,
        layer_input[0],
        cotangent,
        state_in[0].swapaxes(1, 2),
        state_out[0].swapaxes(1, 2),
        step_size[0].swapaxes(1, 2),
        saved_states.reshape(micros, width, states),
        decay_rate,
        skip_gain,
    )
    turned = [part.swapaxes(1, 2)[None] for part in outs[1:4]]
    return (outs[0][None], *turned, outs[4], outs[5])


def solution(mesh):
    layered = P("section", None, "branch", None)
    return jax.shard_map(
        shards,
        mesh=mesh,
        in_specs=(
            layered,
            P(None, "branch", None),
            layered,
            layered,
            layered,
            P("section", None, "branch", None, None, None),
            P("section", None),
            P("section", None),
            P(),
        ),
        out_specs=(
            layered,
            layered,
            layered,
            layered,
            P("section", None),
            P("section", None),
        ),
        check_vma=False,
    )
```
